256 devices in a mesh: mem: 2 (over core), row: 16 (over z_lo, y), col: 8 (over z_hi, x).
Axes of the slice: x: 4, y: 4, z: 8 (z_hi: 2, z_lo: 4; z = z_hi * 4 + z_lo), core: 2. Of those that a mesh axis runs over, the one named last changes fastest.
Arguments:
- tokens: bfloat16 [2048, 2560], P('row', ('mem', 'col')), may hold values from -6 to 6
- cotangent: bfloat16 [2048, 2560], P('row', ('mem', 'col')), may hold values from -3 to 3
- inner_weight: float32 [2, 2560, 6912], P(None, 'row', ('mem', 'col')), may hold values from -0.125 to 0.125
- inner_mean: float32 [2, 2560, 6912], P(None, 'row', ('mem', 'col')), may hold values from -12 to 12
- inner_square: float32 [2, 2560, 6912], P(None, 'row', ('mem', 'col')), may hold values from 2 to 128
- outer_weight: float32 [6912, 2560], P(('mem', 'col'), 'row'), may hold values from -0.078125 to 0.078125
- outer_mean: float32 [6912, 2560], P(('mem', 'col'), 'row'), may hold values from -12 to 12
- outer_square: float32 [6912, 2560], P(('mem', 'col'), 'row'), may hold values from 2 to 128
Outputs:
- token_gradient: bfloat16 [2048, 2560], P('row', ('mem', 'col'))
- inner_stepped: float32 [2, 2560, 6912], P(None, 'row', ('mem', 'col'))
- inner_averaged: float32 [2, 2560, 6912], P(None, 'row', ('mem', 'col'))
- inner_squared: float32 [2, 2560, 6912], P(None, 'row', ('mem', 'col'))
- outer_stepped: float32 [6912, 2560], P(('mem', 'col'), 'row')
- outer_averaged: float32 [6912, 2560], P(('mem', 'col'), 'row')
- outer_squared: float32 [6912, 2560], P(('mem', 'col'), 'row')
The draws below stay inside these ranges and needn't reach their ends.
All inputs are finite; a program needn't handle non-finite values.
Results may differ from the reference program's by a relative error of at most 0.0072.
Values may be sent and summed in bfloat16 or wider, within the bound.
A program may use at most 128 MiB of HBM per device.

```python
import math
import jax
import jax.numpy as jnp

D = 2560
FF = 6912
TOKENS = 2048


def with_spikes(drawn, key, source, target, shards_of, factor):
    owner, partner = [(jnp.arange(drawn.shape[axis_at]) // (drawn.shape[axis_at] // shards_of)).reshape([-1 if axis == axis_at else 1 for axis in range(drawn.ndim)]) for axis_at in (source, target)]
    chosen = jax.random.permutation(key, shards_of)[partner]
    strong = (owner == chosen) | (owner == (partner + shards_of // 2) % shards_of)
    return jnp.where(strong, factor * drawn, drawn)


def block_levels(stream_key, shape, pieces, least, largest):
    factor_of, own = 1.0, jax.random.fold_in(stream_key, 6)
    for axis_at, blocks in pieces:
        heights = jnp.exp(jax.random.uniform(jax.random.fold_in(own, axis_at), (blocks,), jnp.float32, least / len(pieces), largest / len(pieces)))
        factor_of = factor_of * jnp.repeat(heights, shape[axis_at] // blocks).reshape([-1 if axis == axis_at else 1 for axis in range(len(shape))])
    return factor_of


def normal_values(stream_key, dims, scale, bound, cuts=(), kind=jnp.bfloat16):
    array = jax.random.normal(stream_key, dims, jnp.float32) * scale
    if len(cuts) > 0:
        array = block_levels(stream_key, dims, cuts, -0.22, 0.18) * array
    return jnp.clip(array, min=-bound, max=bound).astype(kind)


def gaussian_with(rng, extent, deviation, most, shards, heavy, held_as=jnp.bfloat16):
    entries = deviation * jax.random.normal(rng, extent, jnp.float32)
    if shards:
        entries = entries * block_levels(rng, extent, shards, -0.22, 0.18)
    return jnp.clip(with_spikes(entries, jax.random.fold_in(rng, 3), *heavy), -most, most).astype(held_as)


def setup_inputs(seed: int = 0) -> dict:
    key_of = jax.random.split(jax.random.key(seed), 9)
    tokens = gaussian_with(key_of[0], (TOKENS, D), 1.0, 6.0, ((0, 16), (1, 16)), (0, 1, 16, 2.0))
    cotangent = gaussian_with(key_of[1], (TOKENS, D), 0.5, 3.0, ((0, 16), (1, 16)), (0, 1, 16, 2.0))
    inner_weight = normal_values(key_of[2], (2, D, FF), D ** -0.5, 0.125, ((1, 16), (2, 16)), jnp.float32)
    inner_mean = normal_values(key_of[3], (2, D, FF), 2.0, 12.0, ((1, 16), (2, 16)), jnp.float32)
    inner_square = jnp.clip(jnp.exp(math.log(128.0) - 4.158883 * jax.random.uniform(key_of[4], (2, D, FF), jnp.float32) ** block_levels(key_of[4], (2, D, FF), ((1, 16), (2, 16)), -0.2, 0.2)), 2.0, 128.0)
    outer_weight = normal_values(key_of[5], (FF, D), FF ** -0.5, 0.078125, ((0, 16), (1, 16)), jnp.float32)
    outer_mean = normal_values(key_of[6], (FF, D), 2.0, 12.0, ((0, 16), (1, 16)), jnp.float32)
    outer_square = jnp.clip(jnp.exp(math.log(128.0) - 4.158883 * jax.random.uniform(key_of[7], (FF, D), jnp.float32) ** block_levels(key_of[7], (FF, D), ((0, 16), (1, 16)), -0.2, 0.2)), 2.0, 128.0)
    return {"tokens": tokens, "cotangent": cotangent, "inner_weight": inner_weight, "inner_mean": inner_mean, "inner_square": inner_square, "outer_weight": outer_weight, "outer_mean": outer_mean, "outer_square": outer_square}


beta_one = 0.9
beta_two = 0.95
learn_rate = 0.01
weight_decay = 0.1
epsilon = 1e-08
bias_steps = 20.0

def adam_step(weight, moment, square, gradient):
    moment_next = beta_one * moment + (1.0 - beta_one) * gradient
    square_next = beta_two * square + (1.0 - beta_two) * gradient * gradient
    scaled_moment = moment_next / (1.0 - beta_one ** bias_steps)
    scaled_square = square_next / (1.0 - beta_two ** bias_steps)
    change = scaled_moment / (jnp.sqrt(scaled_square) + epsilon) + weight_decay * weight
    return (weight - learn_rate * change, moment_next, square_next)

def reference(tokens, cotangent, inner_weight, inner_mean, inner_square, outer_weight, outer_mean, outer_square):
    inner_low = inner_weight.astype(jnp.bfloat16)
    outer_low = outer_weight.astype(jnp.bfloat16)
    gating = jnp.dot(tokens, inner_low[0], preferred_element_type=jnp.float32)
    upward = jnp.dot(tokens, inner_low[1], preferred_element_type=jnp.float32)
    logistic = jax.nn.sigmoid(gating)
    hidden = (gating * logistic * upward).astype(jnp.bfloat16)
    hidden_back = jnp.dot(cotangent, outer_low.T, preferred_element_type=jnp.float32)
    gating_back = (hidden_back * upward * logistic * (1.0 + gating * (1.0 - logistic))).astype(jnp.bfloat16)
    upward_back = (hidden_back * gating * logistic).astype(jnp.bfloat16)
    token_gradient = (jnp.dot(gating_back, inner_low[0].T, preferred_element_type=jnp.float32) + jnp.dot(upward_back, inner_low[1].T, preferred_element_type=jnp.float32)).astype(jnp.bfloat16)
    inner_grad = jnp.stack([jnp.dot(tokens.T, gating_back, preferred_element_type=jnp.float32), jnp.dot(tokens.T, upward_back, preferred_element_type=jnp.float32)])
    outer_grad = jnp.dot(hidden.T, cotangent, preferred_element_type=jnp.float32)
    inner_stepped, inner_averaged, inner_squared = adam_step(inner_weight, inner_mean, inner_square, inner_grad)
    outer_stepped, outer_averaged, outer_squared = adam_step(outer_weight, outer_mean, outer_square, outer_grad)
    return (token_gradient, inner_stepped, inner_averaged, inner_squared, outer_stepped, outer_averaged, outer_squared)
```

```python
import functools

import jax
import jax.numpy as jnp
from jax import lax
from jax.experimental import pallas as pl
from jax.experimental.pallas import tpu as pltpu
from jax.sharding import Mesh
from jax.sharding import PartitionSpec as P

MESH = pl.DeviceIdType.MESH
AXES = ("mem", "zl", "y", "zh", "x")
ROW = ("zl", "y")
COL = ("mem", "zh", "x")

beta_one = 0.9
beta_two = 0.95
learn_rate = 0.01
weight_decay = 0.1
epsilon = 1e-08
bias_steps = 20.0

LANES = 128
HOPS = (1, 3, 2)


def chunk_plan(hidden):
    plan, column = [], 0
    for first in range(0, hidden, LANES):
        units = min(LANES, hidden - first)
        pair = -(-2 * units // LANES) * LANES
        plan.append((first, units, column, pair + LANES, pair))
        column += pair + LANES
    return plan, column


def pack_columns(gate, up, outer, plan):
    pieces = []
    for first, units, _, width, pair in plan:
        cut = slice(first, first + units)
        pieces += [gate[:, cut], up[:, cut]]
        if pair > 2 * units:
            pieces.append(jnp.zeros((gate.shape[0], pair - 2 * units), gate.dtype))
        pieces.append(outer[:, cut])
        if width - pair > units:
            pieces.append(jnp.zeros((gate.shape[0], width - pair - units), gate.dtype))
    return jnp.concatenate(pieces, axis=1)


def unpack_columns(packed, plan):
    gate = [packed[:, c : c + n] for _, n, c, _, _ in plan]
    up = [packed[:, c + n : c + 2 * n] for _, n, c, _, _ in plan]
    outer = [packed[:, c + p : c + p + n] for _, n, c, _, p in plan]
    return tuple(jnp.concatenate(parts, axis=1) for parts in (gate, up, outer))


def around(index, hop):
    return lax.rem(index + hop, 4)


def exchange_kernel(plan, x_ref, w_ref, gw_ref, dx_ref, *scratch):
    n = len(plan)
    scratch = list(scratch)

    def take(count):
        taken = scratch[:count]
        del scratch[:count]
        return taken

    xt, xn, dxt, dx_in, dx_out, dx_in2, fin_out, fin_in = take(8)
    wf, pf, ps, pr, act, df, ds, dr = (take(n) for _ in range(8))
    (x1s, x1r, x2s, x2r, x3s, x3r, ws, wr, rs, rr, as_, ar, gs, gr) = take(14)
    (e1s, e1r, e2s, e2r, e3s, e3r) = take(6)

    mem, zl, y, zh, x = (lax.axis_index(a) for a in AXES)
    depth, tokens = x_ref.shape[1:]
    other = 1 - mem
    src_zh, src_mem = lax.rem(zl, 2), zl // 2

    def send(src, dst, send_sem, recv_sem, device):
        copy = pltpu.make_async_remote_copy(
            src_ref=src,
            dst_ref=dst,
            send_sem=send_sem,
            recv_sem=recv_sem,
            device_id=device,
            device_id_type=MESH,
        )
        copy.start()
        sent.append(copy)
        return copy

    sent = []
    spread = [{"zl": mem * 2 + zh, "zh": t, "mem": 1 - zl // 2} for t in range(2)]
    owners = [{"zl": 2 * other + j, "zh": src_zh, "mem": src_mem} for j in range(2)]

    barrier = pltpu.get_barrier_semaphore()
    partners = [{"mem": other}] + spread + owners
    for hop in HOPS:
        partners += [{a: around(i, hop)} for a, i in (("y", y), ("zl", zl), ("x", x))]
    for device in partners:
        pl.semaphore_signal(barrier, inc=1, device_id=device, device_id_type=MESH)
    pl.semaphore_wait(barrier, len(partners))

    def block(zone, part):
        return xt.at[zone, :, pl.ds(pl.multiple_of(part * depth, 16), depth)]

    for t in range(2):
        send(x_ref, block(zl, x), x1s.at[t], x1r.at[lax.rem(zl, 2)], spread[t])

    weights = []
    for k, (_, _, column, width, _) in enumerate(plan):
        columns = pl.ds(column, width)
        weights.append(
            [
                send(w_ref.at[:, columns], wf[k].at[y], ws.at[k, h], wr.at[k, h], {"y": around(y, hop)})
                for h, hop in enumerate(HOPS)
            ]
        )
        wf[k][y] = w_ref[:, column : column + width]

    def arrived(dst, sem):
        pltpu.make_async_copy(dst, dst, sem).wait()

    across = []
    for j in range(2):
        zone = 2 * other + j
        mine = block(zone, x)
        arrived(mine, x1r.at[j])
        across.append(
            [
                send(mine, mine, x2s.at[j, h], x2r.at[j, h], {"x": around(x, hop)})
                for h, hop in enumerate(HOPS)
            ]
        )
        send(mine, mine, x3s.at[j, 3], x3r.at[j, 3], {"mem": other})
    for j in range(2):
        zone = 2 * other + j
        for h, hop in enumerate(HOPS):
            across[j][h].wait_recv()
            theirs = block(zone, around(x, 4 - hop))
            send(theirs, theirs, x3s.at[j, h], x3r.at[j, h], {"mem": other})

    def turn(zone):
        rows = pl.ds(pl.multiple_of(zone * tokens, 128), tokens)
        for a in range(2):
            xn[a, rows, :] = xt[zone, a].T

    for j in range(2):
        turn(2 * other + j)
    for j in range(2):
        zone = 2 * mem + j
        for h, hop in enumerate(HOPS + (0,)):
            arrived(block(zone, around(x, 4 - hop)), x3r.at[j, h])
        turn(zone)

    def forward(k):
        _, _, _, width, pair = plan[k]
        for copy in weights[k]:
            copy.wait_recv()
        w = wf[k][...].reshape(4 * depth, width)
        for a, (low, high) in enumerate(((0, pair), (pair, width))):
            part = jnp.dot(xn[a], w[:, low:high], preferred_element_type=jnp.float32)
            part = part.reshape(4, tokens, high - low)
            pf[k][:, :, low:high] = part
            ps[k][:, :, low:high] = part.astype(jnp.bfloat16)
        return [
            send(ps[k].at[around(zl, hop)], pr[k].at[zl], rs.at[k, h], rr.at[k, h], {"zl": around(zl, hop)})
            for h, hop in enumerate(HOPS)
        ]

    def middle(k, reduced):
        _, units, _, width, pair = plan[k]
        total = pf[k][zl]
        for h, hop in enumerate(HOPS):
            reduced[h].wait_recv()
            total += pr[k][around(zl, 4 - hop)].astype(jnp.float32)
        gating, hidden_back = total[:, :LANES], total[:, pair:]
        whole = units == LANES
        upward = total[:, LANES:pair] if whole else pltpu.roll(gating, LANES - units, 1)
        logistic = 1.0 / (1.0 + jnp.exp(-gating))
        hidden = gating * logistic * upward
        gating_back = hidden_back * upward * logistic * (1.0 + gating * (1.0 - logistic))
        upward_back = hidden_back * gating * logistic
        if whole:
            act[k][zl, :, LANES:pair] = upward_back.astype(jnp.bfloat16)
        else:
            lane = lax.broadcasted_iota(jnp.int32, gating.shape, 1)
            gating_back = jnp.where(
                lane < units,
                gating_back,
                jnp.where(lane < 2 * units, pltpu.roll(upward_back, units, 1), 0.0),
            )
            hidden = jnp.where(lane < units, hidden, 0.0)
        act[k][zl, :, :LANES] = gating_back.astype(jnp.bfloat16)
        act[k][zl, :, pair:] = hidden.astype(jnp.bfloat16)
        return [
            send(act[k].at[zl], act[k].at[zl], as_.at[k, h], ar.at[k, h], {"zl": around(zl, hop)})
            for h, hop in enumerate(HOPS)
        ]

    def backward(k, gathered):
        _, _, _, width, pair = plan[k]
        for copy in gathered:
            copy.wait_recv()
        a = act[k][...].reshape(4 * tokens, width)
        for s, (low, high) in enumerate(((0, pair), (pair, width))):
            turned = jnp.concatenate([xt[zone, s] for zone in range(4)], axis=1)
            part = jnp.dot(turned, a[:, low:high], preferred_element_type=jnp.float32)
            part = part.reshape(4, depth, high - low)
            df[k][:, :, low:high] = part
            ds[k][:, :, low:high] = part.astype(jnp.bfloat16)
        copies = [
            send(ds[k].at[around(y, hop)], dr[k].at[y], gs.at[k, h], gr.at[k, h], {"y": around(y, hop)})
            for h, hop in enumerate(HOPS)
        ]
        w = wf[k][:, :, :pair].reshape(4 * depth, pair)
        for zone in range(4):
            term = lax.dot_general(
                w, act[k][zone, :, :pair], (((1,), (1,)), ((), ())), preferred_element_type=jnp.float32
            )
            dxt[zone] = term if k == 0 else dxt[zone] + term
        return copies

    reduced, gathered, grads = [None] * n, [None] * n, [None] * n
    for step in range(n + 2):
        if step < n:
            reduced[step] = forward(step)
        if 1 <= step < n + 1:
            gathered[step - 1] = middle(step - 1, reduced[step - 1])
        if step >= 2:
            grads[step - 2] = backward(step - 2, gathered[step - 2])

    half = send(dxt.at[pl.ds(2 * mem, 2)], dx_in, e1s, e1r, {"mem": other})

    def gradient(k):
        _, _, column, width, _ = plan[k]
        total = df[k][y]
        for h, hop in enumerate(HOPS):
            grads[k][h].wait_recv()
            total += dr[k][around(y, 4 - hop)].astype(jnp.float32)
        gw_ref[:, column : column + width] = total

    gradient(0)
    half.wait_recv()
    for j in range(2):
        total = dxt[2 * other + j] + dx_in[j]
        dx_in[j] = total
        dx_out[:, j] = total.astype(jnp.bfloat16).reshape(4, depth, tokens)
    pieces = [
        send(dx_out.at[around(x, hop)], dx_in2.at[h], e2s.at[h], e2r.at[h], {"x": around(x, hop)})
        for h, hop in enumerate(HOPS)
    ]
    for k in range(1, n - 1):
        gradient(k)
    for copy in pieces:
        copy.wait_recv()
    rows = pl.ds(pl.multiple_of(x * depth, 16), depth)
    for j in range(2):
        total = dx_in[j, rows, :]
        for h in range(3):
            total += dx_in2[h, j].astype(jnp.float32)
        fin_out[j] = total.astype(jnp.bfloat16)
        send(fin_out.at[j], fin_in.at[zh], e3s.at[j], e3r.at[zh], owners[j])
    gradient(n - 1)
    for t in range(2):
        arrived(fin_in.at[t], e3r.at[t])
    dx_ref[...] = fin_in[0].astype(jnp.float32) + fin_in[1].astype(jnp.float32)
    for copy in sent:
        copy.wait_send()


def exchange(turned, packed, plan):
    _, depth, tokens = turned.shape
    columns = packed.shape[1]
    n = len(plan)
    low, full = jnp.bfloat16, jnp.float32
    widths = [p[3] for p in plan]
    dma = pltpu.SemaphoreType.DMA
    scratch = [
        pltpu.VMEM((4, 2, 4 * depth, tokens), low),
        pltpu.VMEM((2, 4 * tokens, 4 * depth), low),
        pltpu.VMEM((4, 4 * depth, tokens), full),
        pltpu.VMEM((2, 4 * depth, tokens), full),
        pltpu.VMEM((4, 2, depth, tokens), low),
        pltpu.VMEM((3, 2, depth, tokens), low),
        pltpu.VMEM((2, depth, tokens), low),
        pltpu.VMEM((2, depth, tokens), low),
    ]
    for rows, kind in (
        (depth, low),
        (tokens, full),
        (tokens, low),
        (tokens, low),
        (tokens, low),
        (depth, full),
        (depth, low),
        (depth, low),
    ):
        scratch += [pltpu.VMEM((4, rows, width), kind) for width in widths]
    scratch += [dma((2,)), dma((2,)), dma((2, 3)), dma((2, 3)), dma((2, 4)), dma((2, 4))]
    scratch += [dma((n, 3))] * 8
    scratch += [dma, dma, dma((3,)), dma((3,)), dma((2,)), dma((2,))]
    vmem = pl.BlockSpec(memory_space=pltpu.VMEM)
    return pl.pallas_call(
        functools.partial(exchange_kernel, plan),
        out_shape=(
            jax.ShapeDtypeStruct((depth, columns), full),
            jax.ShapeDtypeStruct((depth, tokens), full),
        ),
        in_specs=[vmem, vmem],
        out_specs=(vmem, vmem),
        scratch_shapes=scratch,
        compiler_params=pltpu.CompilerParams(
            collective_id=0, has_side_effects=True, vmem_limit_bytes=56 << 20
        ),
    )(turned, packed)


def adam_step(weight, moment, square, gradient):
    moment_next = beta_one * moment + (1.0 - beta_one) * gradient
    square_next = beta_two * square + (1.0 - beta_two) * gradient * gradient
    scaled_moment = moment_next / (1.0 - beta_one**bias_steps)
    scaled_square = square_next / (1.0 - beta_two**bias_steps)
    change = scaled_moment / (jnp.sqrt(scaled_square) + epsilon) + weight_decay * weight
    return (weight - learn_rate * change, moment_next, square_next)


def on_device(
    tokens,
    cotangent,
    inner_weight,
    inner_mean,
    inner_square,
    outer_weight,
    outer_mean,
    outer_square,
):
    plan, _ = chunk_plan(inner_weight.shape[2])
    inner_low = inner_weight.astype(jnp.bfloat16)
    outer_low = outer_weight.astype(jnp.bfloat16)
    packed = pack_columns(inner_low[0], inner_low[1], outer_low.T, plan)
    turned = jnp.stack([tokens.T, cotangent.T])
    gradient, token_part = exchange(turned, packed, plan)
    token_gradient = token_part.T.astype(jnp.bfloat16)
    gate_gradient, up_gradient, outer_gradient = unpack_columns(gradient, plan)
    inner = adam_step(
        inner_weight, inner_mean, inner_square, jnp.stack([gate_gradient, up_gradient])
    )
    outer = adam_step(outer_weight, outer_mean, outer_square, outer_gradient.T)
    return (token_gradient, *inner, *outer)


def solution(mesh):
    grid = Mesh(mesh.devices.reshape(2, 4, 4, 2, 4), AXES)
    activation, inner, outer = P(ROW, COL), P(None, ROW, COL), P(COL, ROW)
    return jax.shard_map(
        on_device,
        mesh=grid,
        in_specs=(activation, activation, inner, inner, inner, outer, outer, outer),
        out_specs=(activation, inner, inner, inner, outer, outer, outer),
        check_vma=False,
    )
```

```python
import functools

import jax
import jax.numpy as jnp
from jax import lax
from jax.experimental import pallas as pl
from jax.experimental.pallas import tpu as pltpu
from jax.sharding import Mesh
from jax.sharding import PartitionSpec as P

MESH = pl.DeviceIdType.MESH
AXES = ("mem", "zl", "y", "zh", "x")
ROW = ("zl", "y")
COL = ("mem", "zh", "x")

beta_one = 0.9
beta_two = 0.95
learn_rate = 0.01
weight_decay = 0.1
epsilon = 1e-08
bias_steps = 20.0

LANES = 128
HOPS = (1, 3, 2)
ORDER = "F0 F1 F2 R0 F3 R1 M0 R2 M1 G0 R3 M2 G1 B0 M3 G2 B1 G3 B2 B3"


def chunk_plan(hidden):
    plan, column = [], 0
    for first in range(0, hidden, LANES):
        units = min(LANES, hidden - first)
        pair = -(-2 * units // LANES) * LANES
        plan.append((first, units, column, pair + LANES, pair))
        column += pair + LANES
    return plan, column


def pack_columns(gate, up, outer, plan):
    pieces = []
    for first, units, _, width, pair in plan:
        cut = slice(first, first + units)
        pieces += [gate[:, cut], up[:, cut]]
        if pair > 2 * units:
            pieces.append(jnp.zeros((gate.shape[0], pair - 2 * units), gate.dtype))
        pieces.append(outer[:, cut])
        if width - pair > units:
            pieces.append(jnp.zeros((gate.shape[0], width - pair - units), gate.dtype))
    return jnp.concatenate(pieces, axis=1)


def unpack_columns(packed, plan):
    gate = [packed[:, c : c + n] for _, n, c, _, _ in plan]
    up = [packed[:, c + n : c + 2 * n] for _, n, c, _, _ in plan]
    outer = [packed[:, c + p : c + p + n] for _, n, c, _, p in plan]
    return tuple(jnp.concatenate(parts, axis=1) for parts in (gate, up, outer))


def around(index, hop):
    return lax.rem(index + hop, 4)


def exchange_kernel(plan, x_ref, w_ref, gw_ref, dx_ref, *scratch):
    n = len(plan)
    scratch = list(scratch)

    def take(count):
        taken = scratch[:count]
        del scratch[:count]
        return taken

    xt, xn, dxt, dx_in, dx_out, dx_in2, fin_out, fin_in = take(8)
    wf, pf, ps, pr, ps2, act, df, ds, dr = (take(n) for _ in range(9))
    (x1s, x1r, x2s, x2r, x3s, x3r, ws, wr, rs, rr, as_, ar, gs, gr) = take(14)
    (e1s, e1r, e2s, e2r, e3s, e3r) = take(6)

    mem, zl, y, zh, x = (lax.axis_index(a) for a in AXES)
    depth, tokens = x_ref.shape[1:]
    other = 1 - mem
    src_zh, src_mem = lax.rem(zl, 2), zl // 2

    def make(src, dst, send_sem, recv_sem, device):
        return pltpu.make_async_remote_copy(
            src_ref=src,
            dst_ref=dst,
            send_sem=send_sem,
            recv_sem=recv_sem,
            device_id=device,
            device_id_type=MESH,
        )

    def send(*copy):
        copy = make(*copy)
        copy.start()
        sent.append(copy)
        return copy

    sent, sent_middle, sent_end = [], [], []
    is_middle = (zl == 1) | (zl == 2)
    is_end = jnp.logical_not(is_middle)
    left = zl < 2
    near = jnp.where(left, 1 - zl, 5 - zl)
    far_middle, far_end = jnp.where(left, 2, 1), jnp.where(left, 3, 0)
    spread = [{"zl": mem * 2 + zh, "zh": t, "mem": 1 - zl // 2} for t in range(2)]
    owners = [{"zl": 2 * other + j, "zh": src_zh, "mem": src_mem} for j in range(2)]

    barrier = pltpu.get_barrier_semaphore()
    partners = [{"mem": other}] + spread + owners
    for hop in HOPS:
        partners += [{a: around(i, hop)} for a, i in (("y", y), ("zl", zl), ("x", x))]
    for device in partners:
        pl.semaphore_signal(barrier, inc=1, device_id=device, device_id_type=MESH)
    pl.semaphore_wait(barrier, len(partners))

    def block(zone, part):
        return xt.at[zone, :, pl.ds(pl.multiple_of(part * depth, 16), depth)]

    for t in range(2):
        send(x_ref, block(zl, x), x1s.at[t], x1r.at[lax.rem(zl, 2)], spread[t])

    weights = []
    for k, (_, _, column, width, _) in enumerate(plan):
        columns = pl.ds(column, width)
        weights.append(
            [
                send(w_ref.at[:, columns], wf[k].at[y], ws.at[k, h], wr.at[k, h], {"y": around(y, hop)})
                for h, hop in enumerate(HOPS)
            ]
        )
        wf[k][y] = w_ref[:, column : column + width]

    def arrived(dst, sem):
        pltpu.make_async_copy(dst, dst, sem).wait()

    across = []
    for j in range(2):
        zone = 2 * other + j
        mine = block(zone, x)
        arrived(mine, x1r.at[j])
        across.append(
            [
                send(mine, mine, x2s.at[j, h], x2r.at[j, h], {"x": around(x, hop)})
                for h, hop in enumerate(HOPS)
            ]
        )
        send(mine, mine, x3s.at[j, 3], x3r.at[j, 3], {"mem": other})
    for j in range(2):
        zone = 2 * other + j
        for h, hop in enumerate(HOPS):
            across[j][h].wait_recv()
            theirs = block(zone, around(x, 4 - hop))
            send(theirs, theirs, x3s.at[j, h], x3r.at[j, h], {"mem": other})

    def turn(zone):
        rows = pl.ds(pl.multiple_of(zone * tokens, 128), tokens)
        for a in range(2):
            xn[a, rows, :] = xt[zone, a].T

    for j in range(2):
        turn(2 * other + j)
    for j in range(2):
        zone = 2 * mem + j
        for h, hop in enumerate(HOPS + (0,)):
            arrived(block(zone, around(x, 4 - hop)), x3r.at[j, h])
        turn(zone)

    def forward(k):
        _, _, _, width, pair = plan[k]
        for copy in weights[k]:
            copy.wait_recv()
        w = wf[k][...].reshape(4 * depth, width)
        for a, (low, high) in enumerate(((0, pair), (pair, width))):
            part = jnp.dot(xn[a], w[:, low:high], preferred_element_type=jnp.float32)
            part = part.reshape(4, tokens, high - low)
            pf[k][:, :, low:high] = part
            ps[k][:, :, low:high] = part.astype(jnp.bfloat16)
        blocks, inbox = ps[k], pr[k]
        to_near = lambda src, s, slot: make(src, inbox.at[slot], rs.at[k, s], rr.at[k, slot], {"zl": near})
        to_far = lambda src, s, slot: make(src, inbox.at[slot], rs.at[k, s], rr.at[k, slot], {"zl": far_middle})
        from_end = [
            to_near(blocks.at[far_middle], 0, 1),
            to_far(blocks.at[far_end], 1, 2),
            to_near(blocks.at[near], 2, 0),
        ]
        from_middle = [
            to_far(blocks.at[far_end], 0, 3),
            to_far(ps2[k].at[0], 1, 4),
            to_near(ps2[k].at[1], 2, 0),
        ]

        @pl.when(is_end)
        def _():
            for copy in from_end:
                copy.start()

        @pl.when(is_middle)
        def _():
            from_middle[0].start()

        sent_end.extend(from_end)
        sent_middle.extend(from_middle)
        return from_middle

    def relay(k, copies):
        inbox = pr[k]

        @pl.when(is_middle)
        def _():
            arrived(inbox.at[1], rr.at[k, 1])
            total = pf[k][far_middle] + inbox[1].astype(jnp.float32)
            ps2[k][0] = total.astype(jnp.bfloat16)
            copies[1].start()
            arrived(inbox.at[3], rr.at[k, 3])
            arrived(inbox.at[2], rr.at[k, 2])
            total = pf[k][near] + inbox[2].astype(jnp.float32) + inbox[3].astype(jnp.float32)
            ps2[k][1] = total.astype(jnp.bfloat16)
            copies[2].start()

    def middle(k):
        _, units, _, width, pair = plan[k]
        arrived(pr[k].at[0], rr.at[k, 0])
        pf[k][zl] += pr[k][0].astype(jnp.float32)

        @pl.when(is_middle)
        def _():
            arrived(pr[k].at[4], rr.at[k, 4])
            pf[k][zl] += pr[k][4].astype(jnp.float32)

        total = pf[k][zl]
        gating, hidden_back = total[:, :LANES], total[:, pair:]
        whole = units == LANES
        upward = total[:, LANES:pair] if whole else pltpu.roll(gating, LANES - units, 1)
        logistic = 1.0 / (1.0 + jnp.exp(-gating))
        hidden = gating * logistic * upward
        gating_back = hidden_back * upward * logistic * (1.0 + gating * (1.0 - logistic))
        upward_back = hidden_back * gating * logistic
        if whole:
            act[k][zl, :, LANES:pair] = upward_back.astype(jnp.bfloat16)
        else:
            lane = lax.broadcasted_iota(jnp.int32, gating.shape, 1)
            gating_back = jnp.where(
                lane < units,
                gating_back,
                jnp.where(lane < 2 * units, pltpu.roll(upward_back, units, 1), 0.0),
            )
            hidden = jnp.where(lane < units, hidden, 0.0)
        act[k][zl, :, :LANES] = gating_back.astype(jnp.bfloat16)
        act[k][zl, :, pair:] = hidden.astype(jnp.bfloat16)
        mine = act[k].at[zl]
        send(mine, mine, as_.at[k, 0], ar.at[k, 0], {"zl": near})
        send(mine, mine, as_.at[k, 1], ar.at[k, jnp.where(is_middle, 1, 2)], {"zl": far_middle})

    def spread_on(k):
        block_1, block_2 = act[k].at[far_middle], act[k].at[far_end]
        copies = [
            make(block_1, block_1, as_.at[k, 2], ar.at[k, 1], {"zl": near}),
            make(block_2, block_2, as_.at[k, 3], ar.at[k, 2], {"zl": near}),
        ]

        @pl.when(is_middle)
        def _():
            arrived(block_1, ar.at[k, 1])
            copies[0].start()
            arrived(block_2, ar.at[k, 2])
            copies[1].start()

        sent_middle.extend(copies)

    def backward(k):
        _, _, _, width, pair = plan[k]
        arrived(act[k].at[near], ar.at[k, 0])

        @pl.when(is_end)
        def _():
            arrived(act[k].at[far_middle], ar.at[k, 1])
            arrived(act[k].at[far_end], ar.at[k, 2])

        a = act[k][...].reshape(4 * tokens, width)
        for s, (low, high) in enumerate(((0, pair), (pair, width))):
            turned = jnp.concatenate([xt[zone, s] for zone in range(4)], axis=1)
            part = jnp.dot(turned, a[:, low:high], preferred_element_type=jnp.float32)
            part = part.reshape(4, depth, high - low)
            df[k][:, :, low:high] = part
            ds[k][:, :, low:high] = part.astype(jnp.bfloat16)
        copies = [
            send(ds[k].at[around(y, hop)], dr[k].at[y], gs.at[k, h], gr.at[k, h], {"y": around(y, hop)})
            for h, hop in enumerate(HOPS)
        ]
        w = wf[k][:, :, :pair].reshape(4 * depth, pair)
        for zone in range(4):
            term = lax.dot_general(
                w, act[k][zone, :, :pair], (((1,), (1,)), ((), ())), preferred_element_type=jnp.float32
            )
            dxt[zone] = term if k == 0 else dxt[zone] + term
        return copies

    relays, grads = [None] * n, [None] * n
    for stage in ORDER.split():
        kind, k = stage[0], int(stage[1])
        if kind == "F":
            relays[k] = forward(k)
        elif kind == "R":
            relay(k, relays[k])
        elif kind == "M":
            middle(k)
        elif kind == "G":
            spread_on(k)
        else:
            grads[k] = backward(k)

    half = send(dxt.at[pl.ds(2 * mem, 2)], dx_in, e1s, e1r, {"mem": other})

    def gradient(k):
        _, _, column, width, _ = plan[k]
        total = df[k][y]
        for h, hop in enumerate(HOPS):
            grads[k][h].wait_recv()
            total += dr[k][around(y, 4 - hop)].astype(jnp.float32)
        gw_ref[:, column : column + width] = total

    gradient(0)
    half.wait_recv()
    for j in range(2):
        total = dxt[2 * other + j] + dx_in[j]
        dx_in[j] = total
        dx_out[:, j] = total.astype(jnp.bfloat16).reshape(4, depth, tokens)
    pieces = [
        send(dx_out.at[around(x, hop)], dx_in2.at[h], e2s.at[h], e2r.at[h], {"x": around(x, hop)})
        for h, hop in enumerate(HOPS)
    ]
    for k in range(1, n - 1):
        gradient(k)
    for copy in pieces:
        copy.wait_recv()
    rows = pl.ds(pl.multiple_of(x * depth, 16), depth)
    for j in range(2):
        total = dx_in[j, rows, :]
        for h in range(3):
            total += dx_in2[h, j].astype(jnp.float32)
        fin_out[j] = total.astype(jnp.bfloat16)
        send(fin_out.at[j], fin_in.at[zh], e3s.at[j], e3r.at[zh], owners[j])
    gradient(n - 1)
    for t in range(2):
        arrived(fin_in.at[t], e3r.at[t])
    dx_ref[...] = fin_in[0].astype(jnp.float32) + fin_in[1].astype(jnp.float32)
    for copy in sent:
        copy.wait_send()

    @pl.when(is_end)
    def _():
        for copy in sent_end:
            copy.wait_send()

    @pl.when(is_middle)
    def _():
        for copy in sent_middle:
            copy.wait_send()


def exchange(turned, packed, plan):
    _, depth, tokens = turned.shape
    columns = packed.shape[1]
    n = len(plan)
    low, full = jnp.bfloat16, jnp.float32
    widths = [p[3] for p in plan]
    dma = pltpu.SemaphoreType.DMA
    scratch = [
        pltpu.VMEM((4, 2, 4 * depth, tokens), low),
        pltpu.VMEM((2, 4 * tokens, 4 * depth), low),
        pltpu.VMEM((4, 4 * depth, tokens), full),
        pltpu.VMEM((2, 4 * depth, tokens), full),
        pltpu.VMEM((4, 2, depth, tokens), low),
        pltpu.VMEM((3, 2, depth, tokens), low),
        pltpu.VMEM((2, depth, tokens), low),
        pltpu.VMEM((2, depth, tokens), low),
    ]
    for slots, rows, kind in (
        (4, depth, low),
        (4, tokens, full),
        (4, tokens, low),
        (5, tokens, low),
        (2, tokens, low),
        (4, tokens, low),
        (4, depth, full),
        (4, depth, low),
        (4, depth, low),
    ):
        scratch += [pltpu.VMEM((slots, rows, width), kind) for width in widths]
    scratch += [dma((2,)), dma((2,)), dma((2, 3)), dma((2, 3)), dma((2, 4)), dma((2, 4))]
    scratch += [dma((n, count)) for count in (3, 3, 3, 5, 4, 3, 3, 3)]
    scratch += [dma, dma, dma((3,)), dma((3,)), dma((2,)), dma((2,))]
    vmem = pl.BlockSpec(memory_space=pltpu.VMEM)
    return pl.pallas_call(
        functools.partial(exchange_kernel, plan),
        out_shape=(
            jax.ShapeDtypeStruct((depth, columns), full),
            jax.ShapeDtypeStruct((depth, tokens), full),
        ),
        in_specs=[vmem, vmem],
        out_specs=(vmem, vmem),
        scratch_shapes=scratch,
        compiler_params=pltpu.CompilerParams(
            collective_id=0, has_side_effects=True, vmem_limit_bytes=56 << 20
        ),
    )(turned, packed)


def adam_step(weight, moment, square, gradient):
    moment_next = beta_one * moment + (1.0 - beta_one) * gradient
    square_next = beta_two * square + (1.0 - beta_two) * gradient * gradient
    scaled_moment = moment_next / (1.0 - beta_one**bias_steps)
    scaled_square = square_next / (1.0 - beta_two**bias_steps)
    change = scaled_moment / (jnp.sqrt(scaled_square) + epsilon) + weight_decay * weight
    return (weight - learn_rate * change, moment_next, square_next)


def on_device(
    tokens,
    cotangent,
    inner_weight,
    inner_mean,
    inner_square,
    outer_weight,
    outer_mean,
    outer_square,
):
    plan, _ = chunk_plan(inner_weight.shape[2])
    inner_low = inner_weight.astype(jnp.bfloat16)
    outer_low = outer_weight.astype(jnp.bfloat16)
    packed = pack_columns(inner_low[0], inner_low[1], outer_low.T, plan)
    turned = jnp.stack([tokens.T, cotangent.T])
    gradient, token_part = exchange(turned, packed, plan)
    token_gradient = token_part.T.astype(jnp.bfloat16)
    gate_gradient, up_gradient, outer_gradient = unpack_columns(gradient, plan)
    inner = adam_step(
        inner_weight, inner_mean, inner_square, jnp.stack([gate_gradient, up_gradient])
    )
    outer = adam_step(outer_weight, outer_mean, outer_square, outer_gradient.T)
    return (token_gradient, *inner, *outer)


def solution(mesh):
    grid = Mesh(mesh.devices.reshape(2, 4, 4, 2, 4), AXES)
    activation, inner, outer = P(ROW, COL), P(None, ROW, COL), P(COL, ROW)
    return jax.shard_map(
        on_device,
        mesh=grid,
        in_specs=(activation, activation, inner, inner, inner, outer, outer, outer),
        out_specs=(activation, inner, inner, inner, outer, outer, outer),
        check_vma=False,
    )
```

```python
import functools

import jax
import jax.numpy as jnp
from jax import lax
from jax.experimental import pallas as pl
from jax.experimental.pallas import tpu as pltpu
from jax.sharding import Mesh
from jax.sharding import PartitionSpec as P

MESH = pl.DeviceIdType.MESH
AXES = ("mem", "zl", "y", "zh", "x")
ROW = ("zl", "y")
COL = ("mem", "zh", "x")

beta_one = 0.9
beta_two = 0.95
learn_rate = 0.01
weight_decay = 0.1
epsilon = 1e-08
bias_steps = 20.0

LANES = 128
HOPS = (1, 3, 2)
ORDER = "F0 F1 F2 R0 F3 R1 M0 R2 M1 G0 R3 M2 G1 B0 M3 G2 B1 G3 B2 B3"


def chunk_plan(hidden):
    plan = []
    for first in range(0, hidden, LANES):
        units = min(LANES, hidden - first)
        pair = -(-2 * units // LANES) * LANES
        plan.append((first, units, pair + LANES, pair))
    return plan


def around(index, hop):
    return lax.rem(index + hop, 4)


def exchange_kernel(plan, t_ref, c_ref, iw_ref, ow_ref, dx_ref, ig_ref, og_ref, *scratch):
    n = len(plan)
    scratch = list(scratch)

    def take(count):
        taken = scratch[:count]
        del scratch[:count]
        return taken

    x_ref, iw, ow, tile, in_sem = take(5)
    xt, xn, dxt, dx_in, dx_out, dx_in2, fin_out, fin_in = take(8)
    wf, pf, ps, pr, ps2, act, df, ds, dr = (take(n) for _ in range(9))
    (x1s, x1r, x2s, x2r, x3s, x3r, ws, wr, rs, rr, as_, ar, gs, gr) = take(14)
    (e1s, e1r, e2s, e2r, e3s, e3r) = take(6)

    mem, zl, y, zh, x = (lax.axis_index(a) for a in AXES)
    depth, tokens = x_ref.shape[1:]
    other = 1 - mem
    src_zh, src_mem = lax.rem(zl, 2), zl // 2

    def make(src, dst, send_sem, recv_sem, device):
        return pltpu.make_async_remote_copy(
            src_ref=src,
            dst_ref=dst,
            send_sem=send_sem,
            recv_sem=recv_sem,
            device_id=device,
            device_id_type=MESH,
        )

    def send(*copy):
        copy = make(*copy)
        copy.start()
        sent.append(copy)
        return copy

    sent, sent_middle, sent_end = [], [], []
    is_middle = (zl == 1) | (zl == 2)
    is_end = jnp.logical_not(is_middle)
    left = zl < 2
    near = jnp.where(left, 1 - zl, 5 - zl)
    far_middle, far_end = jnp.where(left, 2, 1), jnp.where(left, 3, 0)
    spread = [{"zl": mem * 2 + zh, "zh": t, "mem": 1 - zl // 2} for t in range(2)]
    owners = [{"zl": 2 * other + j, "zh": src_zh, "mem": src_mem} for j in range(2)]

    barrier = pltpu.get_barrier_semaphore()
    partners = [{"mem": other}] + spread + owners
    for hop in HOPS:
        partners += [{a: around(i, hop)} for a, i in (("y", y), ("zl", zl), ("x", x))]
    for device in partners:
        pl.semaphore_signal(barrier, inc=1, device_id=device, device_id_type=MESH)
    loads = [
        pltpu.make_async_copy(src, dst, in_sem.at[i])
        for i, (src, dst) in enumerate(((t_ref, x_ref.at[0]), (c_ref, x_ref.at[1]), (iw_ref, iw), (ow_ref, ow)))
    ]
    for load in loads:
        load.start()
    loads[0].wait()
    loads[1].wait()
    pl.semaphore_wait(barrier, len(partners))

    def block(zone, part):
        return xt.at[zone, :, pl.ds(pl.multiple_of(part * depth, 16), depth)]

    for t in range(2):
        send(x_ref, block(zl, x), x1s.at[t], x1r.at[lax.rem(zl, 2)], spread[t])

    def pack(k):
        first, units, _, pair = plan[k]
        cut = slice(first, first + units)
        if units == LANES:
            wf[k][y, :, :LANES] = iw[0, :, cut].astype(jnp.bfloat16)
            wf[k][y, :, LANES:pair] = iw[1, :, cut].astype(jnp.bfloat16)
            wf[k][y, :, pair:] = ow[:, cut].astype(jnp.bfloat16)
            return
        tile[...] = jnp.zeros_like(tile)
        tile[0, :, :units] = iw[0, :, cut]
        tile[0, :, units : 2 * units] = iw[1, :, cut]
        tile[1, :, :units] = ow[:, cut]
        wf[k][y, :, :pair] = tile[0].astype(jnp.bfloat16)
        wf[k][y, :, pair:] = tile[1].astype(jnp.bfloat16)

    loads[2].wait()
    loads[3].wait()
    weights = []
    for k in range(n):
        pack(k)
        mine = wf[k].at[y]
        weights.append(
            [
                send(mine, mine, ws.at[k, h], wr.at[k, h], {"y": around(y, hop)})
                for h, hop in enumerate(HOPS)
            ]
        )

    def arrived(dst, sem):
        pltpu.make_async_copy(dst, dst, sem).wait()

    across = []
    for j in range(2):
        zone = 2 * other + j
        mine = block(zone, x)
        arrived(mine, x1r.at[j])
        across.append(
            [
                send(mine, mine, x2s.at[j, h], x2r.at[j, h], {"x": around(x, hop)})
                for h, hop in enumerate(HOPS)
            ]
        )
        send(mine, mine, x3s.at[j, 3], x3r.at[j, 3], {"mem": other})
    for j in range(2):
        zone = 2 * other + j
        for h, hop in enumerate(HOPS):
            across[j][h].wait_recv()
            theirs = block(zone, around(x, 4 - hop))
            send(theirs, theirs, x3s.at[j, h], x3r.at[j, h], {"mem": other})

    def turn(zone):
        rows = pl.ds(pl.multiple_of(zone * tokens, 128), tokens)
        for a in range(2):
            xn[a, rows, :] = xt[zone, a].T

    for j in range(2):
        turn(2 * other + j)
    for j in range(2):
        zone = 2 * mem + j
        for h, hop in enumerate(HOPS + (0,)):
            arrived(block(zone, around(x, 4 - hop)), x3r.at[j, h])
        turn(zone)

    def forward(k):
        _, _, width, pair = plan[k]
        for copy in weights[k]:
            copy.wait_recv()
        w = wf[k][...].reshape(4 * depth, width)
        for a, (low, high) in enumerate(((0, pair), (pair, width))):
            part = jnp.dot(xn[a], w[:, low:high], preferred_element_type=jnp.float32)
            part = part.reshape(4, tokens, high - low)
            pf[k][:, :, low:high] = part
            ps[k][:, :, low:high] = part.astype(jnp.bfloat16)
        blocks, inbox = ps[k], pr[k]
        to_near = lambda src, s, slot: make(src, inbox.at[slot], rs.at[k, s], rr.at[k, slot], {"zl": near})
        to_far = lambda src, s, slot: make(src, inbox.at[slot], rs.at[k, s], rr.at[k, slot], {"zl": far_middle})
        from_end = [
            to_near(blocks.at[far_middle], 0, 1),
            to_far(blocks.at[far_end], 1, 2),
            to_near(blocks.at[near], 2, 0),
        ]
        from_middle = [
            to_far(blocks.at[far_end], 0, 3),
            to_far(ps2[k].at[0], 1, 4),
            to_near(ps2[k].at[1], 2, 0),
        ]

        @pl.when(is_end)
        def _():
            for copy in from_end:
                copy.start()

        @pl.when(is_middle)
        def _():
            from_middle[0].start()

        sent_end.extend(from_end)
        sent_middle.extend(from_middle)
        return from_middle

    def relay(k, copies):
        inbox = pr[k]

        @pl.when(is_middle)
        def _():
            arrived(inbox.at[1], rr.at[k, 1])
            total = pf[k][far_middle] + inbox[1].astype(jnp.float32)
            ps2[k][0] = total.astype(jnp.bfloat16)
            copies[1].start()
            arrived(inbox.at[3], rr.at[k, 3])
            arrived(inbox.at[2], rr.at[k, 2])
            total = pf[k][near] + inbox[2].astype(jnp.float32) + inbox[3].astype(jnp.float32)
            ps2[k][1] = total.astype(jnp.bfloat16)
            copies[2].start()

    def middle(k):
        _, units, _, pair = plan[k]
        arrived(pr[k].at[0], rr.at[k, 0])
        pf[k][zl] += pr[k][0].astype(jnp.float32)

        @pl.when(is_middle)
        def _():
            arrived(pr[k].at[4], rr.at[k, 4])
            pf[k][zl] += pr[k][4].astype(jnp.float32)

        total = pf[k][zl]
        gating, hidden_back = total[:, :LANES], total[:, pair:]
        whole = units == LANES
        upward = total[:, LANES:pair] if whole else pltpu.roll(gating, LANES - units, 1)
        logistic = 1.0 / (1.0 + jnp.exp(-gating))
        hidden = gating * logistic * upward
        gating_back = hidden_back * upward * logistic * (1.0 + gating * (1.0 - logistic))
        upward_back = hidden_back * gating * logistic
        if whole:
            act[k][zl, :, LANES:pair] = upward_back.astype(jnp.bfloat16)
        else:
            lane = lax.broadcasted_iota(jnp.int32, gating.shape, 1)
            gating_back = jnp.where(
                lane < units,
                gating_back,
                jnp.where(lane < 2 * units, pltpu.roll(upward_back, units, 1), 0.0),
            )
            hidden = jnp.where(lane < units, hidden, 0.0)
        act[k][zl, :, :LANES] = gating_back.astype(jnp.bfloat16)
        act[k][zl, :, pair:] = hidden.astype(jnp.bfloat16)
        mine = act[k].at[zl]
        send(mine, mine, as_.at[k, 0], ar.at[k, 0], {"zl": near})
        send(mine, mine, as_.at[k, 1], ar.at[k, jnp.where(is_middle, 1, 2)], {"zl": far_middle})

    def spread_on(k):
        block_1, block_2 = act[k].at[far_middle], act[k].at[far_end]
        copies = [
            make(block_1, block_1, as_.at[k, 2], ar.at[k, 1], {"zl": near}),
            make(block_2, block_2, as_.at[k, 3], ar.at[k, 2], {"zl": near}),
        ]

        @pl.when(is_middle)
        def _():
            arrived(block_1, ar.at[k, 1])
            copies[0].start()
            arrived(block_2, ar.at[k, 2])
            copies[1].start()

        sent_middle.extend(copies)

    def backward(k):
        _, _, width, pair = plan[k]
        arrived(act[k].at[near], ar.at[k, 0])

        @pl.when(is_end)
        def _():
            arrived(act[k].at[far_middle], ar.at[k, 1])
            arrived(act[k].at[far_end], ar.at[k, 2])

        a = act[k][...].reshape(4 * tokens, width)
        for s, (low, high) in enumerate(((0, pair), (pair, width))):
            turned = jnp.concatenate([xt[zone, s] for zone in range(4)], axis=1)
            part = jnp.dot(turned, a[:, low:high], preferred_element_type=jnp.float32)
            part = part.reshape(4, depth, high - low)
            df[k][:, :, low:high] = part
            ds[k][:, :, low:high] = part.astype(jnp.bfloat16)
        copies = [
            send(ds[k].at[around(y, hop)], dr[k].at[y], gs.at[k, h], gr.at[k, h], {"y": around(y, hop)})
            for h, hop in enumerate(HOPS)
        ]
        w = wf[k][:, :, :pair].reshape(4 * depth, pair)
        for zone in range(4):
            term = lax.dot_general(
                w, act[k][zone, :, :pair], (((1,), (1,)), ((), ())), preferred_element_type=jnp.float32
            )
            dxt[zone] = term if k == 0 else dxt[zone] + term
        return copies

    relays, grads = [None] * n, [None] * n
    for stage in ORDER.split():
        kind, k = stage[0], int(stage[1])
        if kind == "F":
            relays[k] = forward(k)
        elif kind == "R":
            relay(k, relays[k])
        elif kind == "M":
            middle(k)
        elif kind == "G":
            spread_on(k)
        else:
            grads[k] = backward(k)

    half = send(dxt.at[pl.ds(2 * mem, 2)], dx_in, e1s, e1r, {"mem": other})

    def gradient(k):
        first, units, _, pair = plan[k]
        cut = slice(first, first + units)
        total = df[k][y]
        for h, hop in enumerate(HOPS):
            grads[k][h].wait_recv()
            total += dr[k][around(y, 4 - hop)].astype(jnp.float32)
        ig_ref[0, :, cut] = total[:, :units]
        ig_ref[1, :, cut] = total[:, units : 2 * units]
        og_ref[:, cut] = total[:, pair : pair + units]

    gradient(0)
    half.wait_recv()
    for j in range(2):
        total = dxt[2 * other + j] + dx_in[j]
        dx_in[j] = total
        dx_out[:, j] = total.astype(jnp.bfloat16).reshape(4, depth, tokens)
    pieces = [
        send(dx_out.at[around(x, hop)], dx_in2.at[h], e2s.at[h], e2r.at[h], {"x": around(x, hop)})
        for h, hop in enumerate(HOPS)
    ]
    for k in range(1, n - 1):
        gradient(k)
    for copy in pieces:
        copy.wait_recv()
    rows = pl.ds(pl.multiple_of(x * depth, 16), depth)
    for j in range(2):
        total = dx_in[j, rows, :]
        for h in range(3):
            total += dx_in2[h, j].astype(jnp.float32)
        fin_out[j] = total.astype(jnp.bfloat16)
        send(fin_out.at[j], fin_in.at[zh], e3s.at[j], e3r.at[zh], owners[j])
    gradient(n - 1)
    for t in range(2):
        arrived(fin_in.at[t], e3r.at[t])
    total = fin_in[0].astype(jnp.float32) + fin_in[1].astype(jnp.float32)
    dx_ref[...] = total.astype(jnp.bfloat16)
    for copy in sent:
        copy.wait_send()

    @pl.when(is_end)
    def _():
        for copy in sent_end:
            copy.wait_send()

    @pl.when(is_middle)
    def _():
        for copy in sent_middle:
            copy.wait_send()


def exchange(tokens_block, cotangent_block, inner_weight, outer_weight):
    depth, tokens = tokens_block.shape
    plan = chunk_plan(inner_weight.shape[2])
    n = len(plan)
    low, full = jnp.bfloat16, jnp.float32
    widths = [p[2] for p in plan]
    dma = pltpu.SemaphoreType.DMA
    scratch = [
        pltpu.VMEM((2, depth, tokens), low),
        pltpu.VMEM(inner_weight.shape, full),
        pltpu.VMEM(outer_weight.shape, full),
        pltpu.VMEM((2, depth, LANES), full),
        dma((4,)),
        pltpu.VMEM((4, 2, 4 * depth, tokens), low),
        pltpu.VMEM((2, 4 * tokens, 4 * depth), low),
        pltpu.VMEM((4, 4 * depth, tokens), full),
        pltpu.VMEM((2, 4 * depth, tokens), full),
        pltpu.VMEM((4, 2, depth, tokens), low),
        pltpu.VMEM((3, 2, depth, tokens), low),
        pltpu.VMEM((2, depth, tokens), low),
        pltpu.VMEM((2, depth, tokens), low),
    ]
    for slots, rows, kind in (
        (4, depth, low),
        (4, tokens, full),
        (4, tokens, low),
        (5, tokens, low),
        (2, tokens, low),
        (4, tokens, low),
        (4, depth, full),
        (4, depth, low),
        (4, depth, low),
    ):
        scratch += [pltpu.VMEM((slots, rows, width), kind) for width in widths]
    scratch += [dma((2,)), dma((2,)), dma((2, 3)), dma((2, 3)), dma((2, 4)), dma((2, 4))]
    scratch += [dma((n, count)) for count in (3, 3, 3, 5, 4, 3, 3, 3)]
    scratch += [dma, dma, dma((3,)), dma((3,)), dma((2,)), dma((2,))]
    vmem = pl.BlockSpec(memory_space=pltpu.VMEM)
    hbm = pl.BlockSpec(memory_space=pltpu.HBM)
    return pl.pallas_call(
        functools.partial(exchange_kernel, plan),
        out_shape=(
            jax.ShapeDtypeStruct((depth, tokens), low),
            jax.ShapeDtypeStruct(inner_weight.shape, full),
            jax.ShapeDtypeStruct(outer_weight.shape, full),
        ),
        in_specs=[hbm] * 4,
        out_specs=(vmem,) * 3,
        scratch_shapes=scratch,
        compiler_params=pltpu.CompilerParams(
            collective_id=0, has_side_effects=True, vmem_limit_bytes=56 << 20
        ),
    )(tokens_block, cotangent_block, inner_weight, outer_weight)


def adam_step(weight, moment, square, gradient):
    moment_next = beta_one * moment + (1.0 - beta_one) * gradient
    square_next = beta_two * square + (1.0 - beta_two) * gradient * gradient
    scaled_moment = moment_next / (1.0 - beta_one**bias_steps)
    scaled_square = square_next / (1.0 - beta_two**bias_steps)
    change = scaled_moment / (jnp.sqrt(scaled_square) + epsilon) + weight_decay * weight
    return (weight - learn_rate * change, moment_next, square_next)


def on_device(
    tokens,
    cotangent,
    inner_weight,
    inner_mean,
    inner_square,
    outer_weight,
    outer_mean,
    outer_square,
):
    token_gradient, inner_gradient, outer_gradient = exchange(
        tokens.T, cotangent.T, inner_weight, outer_weight.T
    )
    inner = adam_step(inner_weight, inner_mean, inner_square, inner_gradient)
    outer = adam_step(outer_weight.T, outer_mean.T, outer_square.T, outer_gradient)
    return (token_gradient.T, *inner, *(array.T for array in outer))


def solution(mesh):
    grid = Mesh(mesh.devices.reshape(2, 4, 4, 2, 4), AXES)
    activation, inner, outer = P(ROW, COL), P(None, ROW, COL), P(COL, ROW)
    return jax.shard_map(
        on_device,
        mesh=grid,
        in_specs=(activation, activation, inner, inner, inner, outer, outer, outer),
        out_specs=(activation, inner, inner, inner, outer, outer, outer),
        check_vma=False,
    )
```

```python
import functools

import jax
import jax.numpy as jnp
from jax import lax
from jax.experimental import pallas as pl
from jax.experimental.pallas import tpu as pltpu
from jax.sharding import Mesh
from jax.sharding import PartitionSpec as P

MESH = pl.DeviceIdType.MESH
AXES = ("mem", "zl", "y", "zh", "x")
ROW = ("zl", "y")
COL = ("mem", "zh", "x")

beta_one = 0.9
beta_two = 0.95
learn_rate = 0.01
weight_decay = 0.1
epsilon = 1e-08
bias_steps = 20.0

LANES = 128
HOPS = (1, 3, 2)
EARLY = 2
ORDER = (
    "S0 T0 F0 S1", "F1 T1 H0 H1", "F2 H2 R0 Q0", "F3 H3 R1 Q1", "M0 R2 Q2 M1",
    "R3 Q3 M2 G0", "J0 G1 J1 M3", "U4 U5 G2 J2", "B0 G3 J3 B1", "B2 B3 G4 J4",
    "G5 J5 E0 B4", "B5 E1 D0 D1", "D2 D3 D4 D5",
)


def chunk_plan(hidden):
    plan = []
    for first in range(0, hidden, LANES):
        units = min(LANES, hidden - first)
        pair = -(-2 * units // LANES) * LANES
        plan.append((first, units, pair + LANES, pair))
    return plan


def around(index, hop):
    return lax.rem(index + hop, 4)


def exchange_kernel(plan, t_ref, c_ref, iw_ref, ow_ref, dx_ref, ig_ref, og_ref, *scratch):
    n = len(plan)
    scratch = list(scratch)

    def take(count):
        taken = scratch[:count]
        del scratch[:count]
        return taken

    x_ref, iw, ow, tile, in_sem = take(5)
    xt, xn, dxt, dx_in, dx_out, dx_in2, fin_out, fin_in = take(8)
    wf, pf, ps, pr, ps2 = (take(n) for _ in range(5))
    act, df, ds, dr = (take(n + n // 2) for _ in range(4))
    (x1s, x1r, x2s, x2r, x3s, x3r, ws, wr, rs, rr, as_, ar, gs, gr) = take(14)
    (e1s, e1r, e2s, e2r, e3s, e3r) = take(6)

    mem, zl, y, zh, x = (lax.axis_index(a) for a in AXES)
    depth, tokens = x_ref.shape[1:]
    other = 1 - mem
    src_zh, src_mem = lax.rem(zl, 2), zl // 2

    def make(src, dst, send_sem, recv_sem, device):
        return pltpu.make_async_remote_copy(
            src_ref=src,
            dst_ref=dst,
            send_sem=send_sem,
            recv_sem=recv_sem,
            device_id=device,
            device_id_type=MESH,
        )

    def send(*copy):
        copy = make(*copy)
        copy.start()
        sent.append(copy)
        return copy

    sent, sent_middle, sent_end = [], [], []
    is_middle = (zl == 1) | (zl == 2)
    is_end = jnp.logical_not(is_middle)
    left = zl < 2
    near = jnp.where(left, 1 - zl, 5 - zl)
    far_middle, far_end = jnp.where(left, 2, 1), jnp.where(left, 3, 0)
    spread = [{"zl": mem * 2 + zh, "zh": t, "mem": 1 - zl // 2} for t in range(2)]
    owners = [{"zl": 2 * other + j, "zh": src_zh, "mem": src_mem} for j in range(2)]

    barrier = pltpu.get_barrier_semaphore()
    partners = [{"mem": other}] + spread + owners
    for hop in HOPS:
        partners += [{a: around(i, hop)} for a, i in (("y", y), ("zl", zl), ("x", x))]
    for device in partners:
        pl.semaphore_signal(barrier, inc=1, device_id=device, device_id_type=MESH)
    loads = [
        pltpu.make_async_copy(src, dst, in_sem.at[i])
        for i, (src, dst) in enumerate(((t_ref, x_ref.at[0]), (c_ref, x_ref.at[1]), (iw_ref, iw), (ow_ref, ow)))
    ]
    for load in loads:
        load.start()
    loads[0].wait()
    loads[1].wait()
    pl.semaphore_wait(barrier, len(partners))

    def block(s, zone, part):
        return xt.at[zone, s, pl.ds(pl.multiple_of(part * depth, 16), depth)]

    for s in range(2):
        for t in range(2):
            send(x_ref.at[s], block(s, zl, x), x1s.at[s, t], x1r.at[s, lax.rem(zl, 2)], spread[t])

    def pack(k):
        first, units, _, pair = plan[k]
        cut = slice(first, first + units)
        if units == LANES:
            wf[k][y, :, :LANES] = iw[0, :, cut].astype(jnp.bfloat16)
            wf[k][y, :, LANES:pair] = iw[1, :, cut].astype(jnp.bfloat16)
            wf[k][y, :, pair:] = ow[:, cut].astype(jnp.bfloat16)
            return
        tile[...] = jnp.zeros_like(tile)
        tile[0, :, :units] = iw[0, :, cut]
        tile[0, :, units : 2 * units] = iw[1, :, cut]
        tile[1, :, :units] = ow[:, cut]
        wf[k][y, :, :pair] = tile[0].astype(jnp.bfloat16)
        wf[k][y, :, pair:] = tile[1].astype(jnp.bfloat16)

    loads[2].wait()
    loads[3].wait()
    weights = []
    for k in range(n):
        pack(k)
        mine = wf[k].at[y]
        weights.append(
            [
                send(mine, mine, ws.at[k, h], wr.at[k, h], {"y": around(y, hop)})
                for h, hop in enumerate(HOPS)
            ]
        )

    def arrived(dst, sem):
        pltpu.make_async_copy(dst, dst, sem).wait()

    across = {}
    for s in range(2):
        for j in range(2):
            mine = block(s, 2 * other + j, x)
            arrived(mine, x1r.at[s, j])
            across[s, j] = [
                send(mine, mine, x2s.at[s, j, h], x2r.at[s, j, h], {"x": around(x, hop)})
                for h, hop in enumerate(HOPS)
            ]
            send(mine, mine, x3s.at[s, j, 3], x3r.at[s, j, 3], {"mem": other})

    def share(s):
        for j in range(2):
            for h, hop in enumerate(HOPS):
                across[s, j][h].wait_recv()
                theirs = block(s, 2 * other + j, around(x, 4 - hop))
                send(theirs, theirs, x3s.at[s, j, h], x3r.at[s, j, h], {"mem": other})

    def turn(s):
        def turned(zone):
            rows = pl.ds(pl.multiple_of(zone * tokens, 128), tokens)
            xn[s, rows, :] = xt[zone, s].T

        for j in range(2):
            turned(2 * other + j)
        for j in range(2):
            zone = 2 * mem + j
            for h, hop in enumerate(HOPS + (0,)):
                arrived(block(s, zone, around(x, 4 - hop)), x3r.at[s, j, h])
            turned(zone)

    def parts(k):
        _, _, width, pair = plan[k]
        return [(0, pair), (pair, width)] if k < EARLY else [(0, width)]

    def forward(k, s):
        _, _, width, pair = plan[k]
        if s == 0:
            for copy in weights[k]:
                copy.wait_recv()
        low, high = ((0, pair), (pair, width))[s]
        w = wf[k][:, :, low:high].reshape(4 * depth, high - low)
        part = jnp.dot(xn[s], w, preferred_element_type=jnp.float32)
        part = part.reshape(4, tokens, high - low)
        pf[k][:, :, low:high] = part
        ps[k][:, :, low:high] = part.astype(jnp.bfloat16)
        if k < EARLY:
            begin_sums(k, s)
        elif s == 1:
            begin_sums(k, 0)

    def sums_copy(k, p, src, s, slot, device):
        low, high = parts(k)[p]
        columns = pl.ds(low, high - low)
        return make(
            src.at[:, columns], pr[k].at[slot, :, columns], rs.at[k, p, s], rr.at[k, p, slot], {"zl": device}
        )

    def begin_sums(k, p):
        from_end = [
            sums_copy(k, p, ps[k].at[far_middle], 0, 1, near),
            sums_copy(k, p, ps[k].at[far_end], 1, 2, far_middle),
            sums_copy(k, p, ps[k].at[near], 2, 0, near),
        ]
        from_middle = sums_copy(k, p, ps[k].at[far_end], 0, 3, far_middle)

        @pl.when(is_end)
        def _():
            for copy in from_end:
                copy.start()

        @pl.when(is_middle)
        def _():
            from_middle.start()

        sent_end.extend(from_end)
        sent_middle.append(from_middle)

    def came(k, p, slot):
        low, high = parts(k)[p]
        arrived(pr[k].at[slot, :, pl.ds(low, high - low)], rr.at[k, p, slot])

    def relay(k, first):
        slots, zone, out, target, device = (
            ((1,), far_middle, 0, 4, far_middle) if first else ((3, 2), near, 1, 0, near)
        )
        for p, (low, high) in enumerate(parts(k)):
            copy = sums_copy(k, p, ps2[k].at[out], 1 + out, target, device)

            @pl.when(is_middle)
            def _():
                total = pf[k][zone, :, low:high]
                for slot in slots:
                    came(k, p, slot)
                    total += pr[k][slot, :, low:high].astype(jnp.float32)
                ps2[k][out, :, low:high] = total.astype(jnp.bfloat16)
                copy.start()

            sent_middle.append(copy)

    def middle(k):
        _, units, _, pair = plan[k]
        for p in range(len(parts(k))):
            came(k, p, 0)
        pf[k][zl] += pr[k][0].astype(jnp.float32)

        @pl.when(is_middle)
        def _():
            for p in range(len(parts(k))):
                came(k, p, 4)
            pf[k][zl] += pr[k][4].astype(jnp.float32)

        total = pf[k][zl]
        gating, hidden_back = total[:, :LANES], total[:, pair:]
        whole = units == LANES
        upward = total[:, LANES:pair] if whole else pltpu.roll(gating, LANES - units, 1)
        logistic = 1.0 / (1.0 + jnp.exp(-gating))
        hidden = gating * logistic * upward
        gating_back = hidden_back * upward * logistic * (1.0 + gating * (1.0 - logistic))
        upward_back = hidden_back * gating * logistic
        if whole:
            act[k][zl, :, LANES:pair] = upward_back.astype(jnp.bfloat16)
        else:
            lane = lax.broadcasted_iota(jnp.int32, gating.shape, 1)
            gating_back = jnp.where(
                lane < units,
                gating_back,
                jnp.where(lane < 2 * units, pltpu.roll(upward_back, units, 1), 0.0),
            )
            hidden = jnp.where(lane < units, hidden, 0.0)
        act[k][zl, :, :LANES] = gating_back.astype(jnp.bfloat16)
        first = k % 2 * LANES
        act[n + k // 2][zl, :, first : first + LANES] = hidden.astype(jnp.bfloat16)
        give(k)

    def give(i):
        mine = act[i].at[zl]
        send(mine, mine, as_.at[i, 0], ar.at[i, 0], {"zl": near})
        send(mine, mine, as_.at[i, 1], ar.at[i, jnp.where(is_middle, 1, 2)], {"zl": far_middle})

    def pass_on(k, first):
        zone, slot = (far_middle, 1) if first else (far_end, 2)
        held = act[k].at[zone]
        copy = make(held, held, as_.at[k, 1 + slot], ar.at[k, slot], {"zl": near})

        @pl.when(is_middle)
        def _():
            arrived(held, ar.at[k, slot])
            copy.start()

        sent_middle.append(copy)

    def backward(i):
        arrived(act[i].at[near], ar.at[i, 0])

        @pl.when(is_end)
        def _():
            arrived(act[i].at[far_middle], ar.at[i, 1])
            arrived(act[i].at[far_end], ar.at[i, 2])

        width = act[i].shape[2]

        def token_part():
            w = wf[i][:, :, :width].reshape(4 * depth, width)
            for zone in range(4):
                term = lax.dot_general(
                    w, act[i][zone], (((1,), (1,)), ((), ())), preferred_element_type=jnp.float32
                )
                dxt[zone] = term if i == 0 else dxt[zone] + term

        half = None
        if i == n - 1:
            token_part()
            half = [
                send(dxt.at[2 * mem + j], dx_in.at[j], e1s.at[j], e1r.at[j], {"mem": other}) for j in range(2)
            ]
        turned = jnp.concatenate([xt[zone, int(i >= n)] for zone in range(4)], axis=1)
        part = jnp.dot(turned, act[i][...].reshape(4 * tokens, width), preferred_element_type=jnp.float32)
        part = part.reshape(4, depth, width)
        df[i][...] = part
        ds[i][...] = part.astype(jnp.bfloat16)
        grads[i] = [
            send(ds[i].at[around(y, hop)], dr[i].at[y], gs.at[i, h], gr.at[i, h], {"y": around(y, hop)})
            for h, hop in enumerate(HOPS)
        ]
        if i < n - 1:
            token_part()
        return half

    def gradient(i):
        total = df[i][y]
        for h, hop in enumerate(HOPS):
            grads[i][h].wait_recv()
            total += dr[i][around(y, 4 - hop)].astype(jnp.float32)
        if i < n:
            first, units, _, _ = plan[i]
            ig_ref[0, :, first : first + units] = total[:, :units]
            ig_ref[1, :, first : first + units] = total[:, units : 2 * units]
            return
        for k in range(2 * (i - n), min(2 * (i - n) + 2, n)):
            first, units, _, _ = plan[k]
            low = k % 2 * LANES
            og_ref[:, first : first + units] = total[:, low : low + units]

    def along_x():
        for j in range(2):
            half[j].wait_recv()
            total = dxt[2 * other + j] + dx_in[j]
            dx_in[j] = total
            dx_out[:, j] = total.astype(jnp.bfloat16).reshape(4, depth, tokens)
            pieces.append(
                [
                    send(
                        dx_out.at[around(x, hop), j], dx_in2.at[h, j], e2s.at[j, h], e2r.at[j, h], {"x": around(x, hop)}
                    )
                    for h, hop in enumerate(HOPS)
                ]
            )

    def home():
        rows = pl.ds(pl.multiple_of(x * depth, 16), depth)
        for j in range(2):
            total = dx_in[j, rows, :]
            for h in range(3):
                pieces[j][h].wait_recv()
                total += dx_in2[h, j].astype(jnp.float32)
            fin_out[j] = total.astype(jnp.bfloat16)
            send(fin_out.at[j], fin_in.at[zh], e3s.at[j], e3r.at[zh], owners[j])

    grads, half, pieces = [None] * (n + n // 2), None, []
    for stage in [step for steps in ORDER for step in steps.split()]:
        kind, k = stage[0], int(stage[1])
        if kind == "S":
            share(k)
        elif kind == "T":
            turn(k)
        elif kind in "FH":
            forward(k, "FH".index(kind))
        elif kind in "RQ":
            relay(k, kind == "R")
        elif kind == "M":
            middle(k)
        elif kind == "U":
            give(k)
        elif kind in "GJ":
            pass_on(k, kind == "G")
        elif kind == "B":
            half = backward(k) or half
        elif kind == "E":
            (along_x, home)[k]()
        else:
            gradient(k)
    for t in range(2):
        arrived(fin_in.at[t], e3r.at[t])
    total = fin_in[0].astype(jnp.float32) + fin_in[1].astype(jnp.float32)
    dx_ref[...] = total.astype(jnp.bfloat16)
    for copy in sent:
        copy.wait_send()

    @pl.when(is_end)
    def _():
        for copy in sent_end:
            copy.wait_send()

    @pl.when(is_middle)
    def _():
        for copy in sent_middle:
            copy.wait_send()


def exchange(tokens_block, cotangent_block, inner_weight, outer_weight):
    depth, tokens = tokens_block.shape
    plan = chunk_plan(inner_weight.shape[2])
    n = len(plan)
    low, full = jnp.bfloat16, jnp.float32
    widths = [p[2] for p in plan]
    dma = pltpu.SemaphoreType.DMA
    scratch = [
        pltpu.VMEM((2, depth, tokens), low),
        pltpu.VMEM(inner_weight.shape, full),
        pltpu.VMEM(outer_weight.shape, full),
        pltpu.VMEM((2, depth, LANES), full),
        dma((4,)),
        pltpu.VMEM((4, 2, 4 * depth, tokens), low),
        pltpu.VMEM((2, 4 * tokens, 4 * depth), low),
        pltpu.VMEM((4, 4 * depth, tokens), full),
        pltpu.VMEM((2, 4 * depth, tokens), full),
        pltpu.VMEM((4, 2, depth, tokens), low),
        pltpu.VMEM((3, 2, depth, tokens), low),
        pltpu.VMEM((2, depth, tokens), low),
        pltpu.VMEM((2, depth, tokens), low),
    ]
    for slots, rows, kind in (
        (4, depth, low),
        (4, tokens, full),
        (4, tokens, low),
        (5, tokens, low),
        (2, tokens, low),
    ):
        scratch += [pltpu.VMEM((slots, rows, width), kind) for width in widths]
    widths = [p[3] for p in plan] + [2 * LANES] * (n // 2)
    for rows, kind in ((tokens, low), (depth, full), (depth, low), (depth, low)):
        scratch += [pltpu.VMEM((4, rows, width), kind) for width in widths]
    scratch += [dma((2, 2)), dma((2, 2)), dma((2, 2, 3)), dma((2, 2, 3)), dma((2, 2, 4)), dma((2, 2, 4))]
    scratch += [dma((n, 3)), dma((n, 3)), dma((n, 2, 3)), dma((n, 2, 5))]
    scratch += [dma((n + n // 2, count)) for count in (4, 3, 3, 3)]
    scratch += [dma((2,)), dma((2,)), dma((2, 3)), dma((2, 3)), dma((2,)), dma((2,))]
    vmem = pl.BlockSpec(memory_space=pltpu.VMEM)
    hbm = pl.BlockSpec(memory_space=pltpu.HBM)
    return pl.pallas_call(
        functools.partial(exchange_kernel, plan),
        out_shape=(
            jax.ShapeDtypeStruct((depth, tokens), low),
            jax.ShapeDtypeStruct(inner_weight.shape, full),
            jax.ShapeDtypeStruct(outer_weight.shape, full),
        ),
        in_specs=[hbm] * 4,
        out_specs=(vmem,) * 3,
        scratch_shapes=scratch,
        compiler_params=pltpu.CompilerParams(
            collective_id=0, has_side_effects=True, vmem_limit_bytes=56 << 20
        ),
    )(tokens_block, cotangent_block, inner_weight, outer_weight)


def adam_step(weight, moment, square, gradient):
    moment_next = beta_one * moment + (1.0 - beta_one) * gradient
    square_next = beta_two * square + (1.0 - beta_two) * gradient * gradient
    scaled_moment = moment_next / (1.0 - beta_one**bias_steps)
    scaled_square = square_next / (1.0 - beta_two**bias_steps)
    change = scaled_moment / (jnp.sqrt(scaled_square) + epsilon) + weight_decay * weight
    return (weight - learn_rate * change, moment_next, square_next)


def on_device(
    tokens,
    cotangent,
    inner_weight,
    inner_mean,
    inner_square,
    outer_weight,
    outer_mean,
    outer_square,
):
    token_gradient, inner_gradient, outer_gradient = exchange(
        tokens.T, cotangent.T, inner_weight, outer_weight.T
    )
    inner = adam_step(inner_weight, inner_mean, inner_square, inner_gradient)
    outer = adam_step(outer_weight.T, outer_mean.T, outer_square.T, outer_gradient)
    return (token_gradient.T, *inner, *(array.T for array in outer))


def solution(mesh):
    grid = Mesh(mesh.devices.reshape(2, 4, 4, 2, 4), AXES)
    activation, inner, outer = P(ROW, COL), P(None, ROW, COL), P(COL, ROW)
    return jax.shard_map(
        on_device,
        mesh=grid,
        in_specs=(activation, activation, inner, inner, inner, outer, outer, outer),
        out_specs=(activation, inner, inner, inner, outer, outer, outer),
        check_vma=False,
    )
```

```python
import functools

import jax
import jax.numpy as jnp
from jax import lax
from jax.experimental import pallas as pl
from jax.experimental.pallas import tpu as pltpu
from jax.sharding import Mesh
from jax.sharding import PartitionSpec as P

MESH = pl.DeviceIdType.MESH
AXES = ("mem", "zl", "y", "zh", "x")
ROW = ("zl", "y")
COL = ("mem", "zh", "x")

beta_one = 0.9
beta_two = 0.95
learn_rate = 0.01
weight_decay = 0.1
epsilon = 1e-08
bias_steps = 20.0

LANES = 128
HOPS = (1, 3, 2)
EARLY = 2
ORDER = (
    "S0 T0 F0 S1", "F1 T1 H0 H1", "F2 H2 R0 Q0", "F3 H3 R1 Q1", "M0 R2 Q2 M1",
    "R3 Q3 M2 G0", "J0 G1 J1 M3", "U4 U5 G2 J2", "B0 G3 J3 B1", "B2 B3 G4 J4",
    "G5 J5 E0 B4", "B5 E1 D0 D1", "D2 D3 D4 D5",
)


def chunk_plan(hidden):
    plan = []
    for first in range(0, hidden, LANES):
        units = min(LANES, hidden - first)
        pair = -(-2 * units // LANES) * LANES
        plan.append((first, units, pair + LANES, pair))
    return plan


def around(index, hop):
    return lax.rem(index + hop, 4)


def exchange_kernel(plan, t_ref, c_ref, iw_ref, ow_ref, dx_ref, ig_ref, og_ref, *scratch):
    n = len(plan)
    scratch = list(scratch)

    def take(count):
        taken = scratch[:count]
        del scratch[:count]
        return taken

    x_ref, iw, ow, tile, in_sem = take(5)
    xt, xn, dxt, dx_in, dx_out, dx_in2, fin_out, fin_in = take(8)
    wf, pf, ps, pr, ps2 = (take(n) for _ in range(5))
    act, df, ds, dr = (take(n + n // 2) for _ in range(4))
    (x1s, x1r, x2s, x2r, x3s, x3r, ws, wr, rs, rr, as_, ar, gs, gr) = take(14)
    (e1s, e1r, e2s, e2r, e3s, e3r) = take(6)

    mem, zl, y, zh, x = (lax.axis_index(a) for a in AXES)
    depth, tokens = x_ref.shape[1:]
    other = 1 - mem
    src_zh, src_mem = lax.rem(zl, 2), zl // 2

    def make(src, dst, send_sem, recv_sem, device):
        return pltpu.make_async_remote_copy(
            src_ref=src,
            dst_ref=dst,
            send_sem=send_sem,
            recv_sem=recv_sem,
            device_id=device,
            device_id_type=MESH,
        )

    def send(*copy):
        copy = make(*copy)
        copy.start()
        sent.append(copy)
        return copy

    sent, sent_middle, sent_end = [], [], []
    is_middle = (zl == 1) | (zl == 2)
    is_end = jnp.logical_not(is_middle)
    left = zl < 2
    near = jnp.where(left, 1 - zl, 5 - zl)
    far_middle, far_end = jnp.where(left, 2, 1), jnp.where(left, 3, 0)
    spread = [{"zl": mem * 2 + zh, "zh": t, "mem": 1 - zl // 2} for t in range(2)]
    owners = [{"zl": 2 * other + j, "zh": src_zh, "mem": src_mem} for j in range(2)]

    barrier = pltpu.get_barrier_semaphore()
    partners = [{"mem": other}] + spread + owners
    for hop in HOPS:
        partners += [{a: around(i, hop)} for a, i in (("y", y), ("zl", zl), ("x", x))]
    for device in partners:
        pl.semaphore_signal(barrier, inc=1, device_id=device, device_id_type=MESH)
    loads = [
        pltpu.make_async_copy(src, dst, in_sem.at[i])
        for i, (src, dst) in enumerate(((t_ref, x_ref.at[0]), (c_ref, x_ref.at[1]), (iw_ref, iw), (ow_ref, ow)))
    ]
    for load in loads:
        load.start()
    loads[0].wait()
    loads[1].wait()
    pl.semaphore_wait(barrier, len(partners))

    def block(s, zone, part):
        return xt.at[zone, s, pl.ds(pl.multiple_of(part * depth, 16), depth)]

    for s in range(2):
        for t in range(2):
            send(x_ref.at[s], block(s, zl, x), x1s.at[s, t], x1r.at[s, lax.rem(zl, 2)], spread[t])

    def pack(k):
        first, units, _, pair = plan[k]
        cut = slice(first, first + units)
        if units == LANES:
            wf[k][y, :, :LANES] = iw[0, :, cut].astype(jnp.bfloat16)
            wf[k][y, :, LANES:pair] = iw[1, :, cut].astype(jnp.bfloat16)
            wf[k][y, :, pair:] = ow[:, cut].astype(jnp.bfloat16)
            return
        tile[...] = jnp.zeros_like(tile)
        tile[0, :, :units] = iw[0, :, cut]
        tile[0, :, units : 2 * units] = iw[1, :, cut]
        tile[1, :, :units] = ow[:, cut]
        wf[k][y, :, :pair] = tile[0].astype(jnp.bfloat16)
        wf[k][y, :, pair:] = tile[1].astype(jnp.bfloat16)

    loads[2].wait()
    loads[3].wait()
    weights = []
    for k in range(n):
        pack(k)
        mine = wf[k].at[y]
        weights.append(
            [
                send(mine, mine, ws.at[k, h], wr.at[k, h], {"y": around(y, hop)})
                for h, hop in enumerate(HOPS)
            ]
        )

    def arrived(dst, sem):
        pltpu.make_async_copy(dst, dst, sem).wait()

    across = {}
    for s in range(2):
        for j in range(2):
            mine = block(s, 2 * other + j, x)
            arrived(mine, x1r.at[s, j])
            across[s, j] = [
                send(mine, mine, x2s.at[s, j, h], x2r.at[s, j, h], {"x": around(x, hop)})
                for h, hop in enumerate(HOPS)
            ]
            send(mine, mine, x3s.at[s, j, 3], x3r.at[s, j, 3], {"mem": other})

    def share(s):
        for j in range(2):
            for h, hop in enumerate(HOPS):
                across[s, j][h].wait_recv()
                theirs = block(s, 2 * other + j, around(x, 4 - hop))
                send(theirs, theirs, x3s.at[s, j, h], x3r.at[s, j, h], {"mem": other})

    def turn(s):
        def turned(zone):
            rows = pl.ds(pl.multiple_of(zone * tokens, 128), tokens)
            xn[s, rows, :] = xt[zone, s].T

        for j in range(2):
            turned(2 * other + j)
        for j in range(2):
            zone = 2 * mem + j
            for h, hop in enumerate(HOPS + (0,)):
                arrived(block(s, zone, around(x, 4 - hop)), x3r.at[s, j, h])
            turned(zone)

    def parts(k):
        _, _, width, pair = plan[k]
        return [(0, pair), (pair, width)] if k < EARLY else [(0, width)]

    def forward(k, s):
        _, _, width, pair = plan[k]
        if s == 0:
            for copy in weights[k]:
                copy.wait_recv()
        low, high = ((0, pair), (pair, width))[s]
        w = wf[k][:, :, low:high].reshape(4 * depth, high - low)
        part = jnp.dot(xn[s], w, preferred_element_type=jnp.float32)
        part = part.reshape(4, tokens, high - low)
        pf[k][:, :, low:high] = part
        ps[k][:, :, low:high] = part.astype(jnp.bfloat16)
        if k < EARLY:
            begin_sums(k, s)
        elif s == 1:
            begin_sums(k, 0)

    def sums_copy(k, p, src, s, slot, device):
        low, high = parts(k)[p]
        columns = pl.ds(low, high - low)
        return make(
            src.at[:, columns], pr[k].at[slot, :, columns], rs.at[k, p, s], rr.at[k, p, slot], {"zl": device}
        )

    def begin_sums(k, p):
        from_end = [
            sums_copy(k, p, ps[k].at[far_middle], 0, 1, near),
            sums_copy(k, p, ps[k].at[far_end], 1, 2, far_middle),
            sums_copy(k, p, ps[k].at[near], 2, 0, near),
        ]
        from_middle = sums_copy(k, p, ps[k].at[far_end], 0, 3, far_middle)

        @pl.when(is_end)
        def _():
            for copy in from_end:
                copy.start()

        @pl.when(is_middle)
        def _():
            from_middle.start()

        sent_end.extend(from_end)
        sent_middle.append(from_middle)

    def came(k, p, slot):
        low, high = parts(k)[p]
        arrived(pr[k].at[slot, :, pl.ds(low, high - low)], rr.at[k, p, slot])

    def relay(k, first):
        slots, zone, out, target, device = (
            ((1,), far_middle, 0, 4, far_middle) if first else ((3, 2), near, 1, 0, near)
        )
        for p, (low, high) in enumerate(parts(k)):
            copy = sums_copy(k, p, ps2[k].at[out], 1 + out, target, device)

            @pl.when(is_middle)
            def _():
                total = pf[k][zone, :, low:high]
                for slot in slots:
                    came(k, p, slot)
                    total += pr[k][slot, :, low:high].astype(jnp.float32)
                ps2[k][out, :, low:high] = total.astype(jnp.bfloat16)
                copy.start()

            sent_middle.append(copy)

    def middle(k):
        _, units, _, pair = plan[k]
        for p in range(len(parts(k))):
            came(k, p, 0)
        pf[k][zl] += pr[k][0].astype(jnp.float32)

        @pl.when(is_middle)
        def _():
            for p in range(len(parts(k))):
                came(k, p, 4)
            pf[k][zl] += pr[k][4].astype(jnp.float32)

        total = pf[k][zl]
        gating, hidden_back = total[:, :LANES], total[:, pair:]
        whole = units == LANES
        upward = total[:, LANES:pair] if whole else pltpu.roll(gating, LANES - units, 1)
        logistic = 1.0 / (1.0 + jnp.exp(-gating))
        hidden = gating * logistic * upward
        gating_back = hidden_back * upward * logistic * (1.0 + gating * (1.0 - logistic))
        upward_back = hidden_back * gating * logistic
        if whole:
            act[k][zl, :, LANES:pair] = upward_back.astype(jnp.bfloat16)
        else:
            lane = lax.broadcasted_iota(jnp.int32, gating.shape, 1)
            gating_back = jnp.where(
                lane < units,
                gating_back,
                jnp.where(lane < 2 * units, pltpu.roll(upward_back, units, 1), 0.0),
            )
            hidden = jnp.where(lane < units, hidden, 0.0)
        act[k][zl, :, :LANES] = gating_back.astype(jnp.bfloat16)
        first = k % 2 * LANES
        act[n + k // 2][zl, :, first : first + LANES] = hidden.astype(jnp.bfloat16)
        give(k)

    def give(i):
        mine = act[i].at[zl]
        send(mine, mine, as_.at[i, 0], ar.at[i, 0], {"zl": near})
        send(mine, mine, as_.at[i, 1], ar.at[i, jnp.where(is_middle, 1, 2)], {"zl": far_middle})

    def pass_on(k, first):
        zone, slot = (far_middle, 1) if first else (far_end, 2)
        held = act[k].at[zone]
        copy = make(held, held, as_.at[k, 1 + slot], ar.at[k, slot], {"zl": near})

        @pl.when(is_middle)
        def _():
            arrived(held, ar.at[k, slot])
            copy.start()

        sent_middle.append(copy)

    def backward(i):
        arrived(act[i].at[near], ar.at[i, 0])

        @pl.when(is_end)
        def _():
            arrived(act[i].at[far_middle], ar.at[i, 1])
            arrived(act[i].at[far_end], ar.at[i, 2])

        width = act[i].shape[2]

        def token_part():
            w = wf[i][:, :, :width].reshape(4 * depth, width)
            copies = []
            for j, zone in enumerate((2 * mem, 2 * mem + 1, 2 * other, 2 * other + 1) if i == n - 1 else range(4)):
                term = lax.dot_general(
                    w, act[i][zone], (((1,), (1,)), ((), ())), preferred_element_type=jnp.float32
                )
                dxt[zone] = term if i == 0 else dxt[zone] + term
                if i == n - 1 and j < 2:
                    copies.append(send(dxt.at[zone], dx_in.at[j], e1s.at[j], e1r.at[j], {"mem": other}))
            return copies

        half = None
        if i == n - 1:
            half = token_part()
        turned = jnp.concatenate([xt[zone, int(i >= n)] for zone in range(4)], axis=1)
        part = jnp.dot(turned, act[i][...].reshape(4 * tokens, width), preferred_element_type=jnp.float32)
        part = part.reshape(4, depth, width)
        df[i][...] = part
        ds[i][...] = part.astype(jnp.bfloat16)
        grads[i] = [
            send(ds[i].at[around(y, hop)], dr[i].at[y], gs.at[i, h], gr.at[i, h], {"y": around(y, hop)})
            for h, hop in enumerate(HOPS)
        ]
        if i < n - 1:
            token_part()
        return half

    def gradient(i):
        total = df[i][y]
        for h, hop in enumerate(HOPS):
            grads[i][h].wait_recv()
            total += dr[i][around(y, 4 - hop)].astype(jnp.float32)
        if i < n:
            first, units, _, _ = plan[i]
            ig_ref[0, :, first : first + units] = total[:, :units]
            ig_ref[1, :, first : first + units] = total[:, units : 2 * units]
            return
        for k in range(2 * (i - n), min(2 * (i - n) + 2, n)):
            first, units, _, _ = plan[k]
            low = k % 2 * LANES
            og_ref[:, first : first + units] = total[:, low : low + units]

    def along_x():
        for j in range(2):
            half[j].wait_recv()
            total = dxt[2 * other + j] + dx_in[j]
            dx_in[j] = total
            dx_out[:, j] = total.astype(jnp.bfloat16).reshape(4, depth, tokens)
            pieces.append(
                [
                    send(
                        dx_out.at[around(x, hop), j], dx_in2.at[h, j], e2s.at[j, h], e2r.at[j, h], {"x": around(x, hop)}
                    )
                    for h, hop in enumerate(HOPS)
                ]
            )

    def home():
        rows = pl.ds(pl.multiple_of(x * depth, 16), depth)
        for j in range(2):
            total = dx_in[j, rows, :]
            for h in range(3):
                pieces[j][h].wait_recv()
                total += dx_in2[h, j].astype(jnp.float32)
            fin_out[j] = total.astype(jnp.bfloat16)
            send(fin_out.at[j], fin_in.at[zh], e3s.at[j], e3r.at[zh], owners[j])

    grads, half, pieces = [None] * (n + n // 2), None, []
    for stage in [step for steps in ORDER for step in steps.split()]:
        kind, k = stage[0], int(stage[1])
        if kind == "S":
            share(k)
        elif kind == "T":
            turn(k)
        elif kind in "FH":
            forward(k, "FH".index(kind))
        elif kind in "RQ":
            relay(k, kind == "R")
        elif kind == "M":
            middle(k)
        elif kind == "U":
            give(k)
        elif kind in "GJ":
            pass_on(k, kind == "G")
        elif kind == "B":
            half = backward(k) or half
        elif kind == "E":
            (along_x, home)[k]()
        else:
            gradient(k)
    for t in range(2):
        arrived(fin_in.at[t], e3r.at[t])
    total = fin_in[0].astype(jnp.float32) + fin_in[1].astype(jnp.float32)
    dx_ref[...] = total.astype(jnp.bfloat16)
    for copy in sent:
        copy.wait_send()

    @pl.when(is_end)
    def _():
        for copy in sent_end:
            copy.wait_send()

    @pl.when(is_middle)
    def _():
        for copy in sent_middle:
            copy.wait_send()


def exchange(tokens_block, cotangent_block, inner_weight, outer_weight):
    depth, tokens = tokens_block.shape
    plan = chunk_plan(inner_weight.shape[2])
    n = len(plan)
    low, full = jnp.bfloat16, jnp.float32
    widths = [p[2] for p in plan]
    dma = pltpu.SemaphoreType.DMA
    scratch = [
        pltpu.VMEM((2, depth, tokens), low),
        pltpu.VMEM(inner_weight.shape, full),
        pltpu.VMEM(outer_weight.shape, full),
        pltpu.VMEM((2, depth, LANES), full),
        dma((4,)),
        pltpu.VMEM((4, 2, 4 * depth, tokens), low),
        pltpu.VMEM((2, 4 * tokens, 4 * depth), low),
        pltpu.VMEM((4, 4 * depth, tokens), full),
        pltpu.VMEM((2, 4 * depth, tokens), full),
        pltpu.VMEM((4, 2, depth, tokens), low),
        pltpu.VMEM((3, 2, depth, tokens), low),
        pltpu.VMEM((2, depth, tokens), low),
        pltpu.VMEM((2, depth, tokens), low),
    ]
    for slots, rows, kind in (
        (4, depth, low),
        (4, tokens, full),
        (4, tokens, low),
        (5, tokens, low),
        (2, tokens, low),
    ):
        scratch += [pltpu.VMEM((slots, rows, width), kind) for width in widths]
    widths = [p[3] for p in plan] + [2 * LANES] * (n // 2)
    for rows, kind in ((tokens, low), (depth, full), (depth, low), (depth, low)):
        scratch += [pltpu.VMEM((4, rows, width), kind) for width in widths]
    scratch += [dma((2, 2)), dma((2, 2)), dma((2, 2, 3)), dma((2, 2, 3)), dma((2, 2, 4)), dma((2, 2, 4))]
    scratch += [dma((n, 3)), dma((n, 3)), dma((n, 2, 3)), dma((n, 2, 5))]
    scratch += [dma((n + n // 2, count)) for count in (4, 3, 3, 3)]
    scratch += [dma((2,)), dma((2,)), dma((2, 3)), dma((2, 3)), dma((2,)), dma((2,))]
    vmem = pl.BlockSpec(memory_space=pltpu.VMEM)
    hbm = pl.BlockSpec(memory_space=pltpu.HBM)
    return pl.pallas_call(
        functools.partial(exchange_kernel, plan),
        out_shape=(
            jax.ShapeDtypeStruct((depth, tokens), low),
            jax.ShapeDtypeStruct(inner_weight.shape, full),
            jax.ShapeDtypeStruct(outer_weight.shape, full),
        ),
        in_specs=[hbm] * 4,
        out_specs=(vmem,) * 3,
        scratch_shapes=scratch,
        compiler_params=pltpu.CompilerParams(
            collective_id=0, has_side_effects=True, vmem_limit_bytes=56 << 20
        ),
    )(tokens_block, cotangent_block, inner_weight, outer_weight)


def adam_step(weight, moment, square, gradient):
    moment_next = beta_one * moment + (1.0 - beta_one) * gradient
    square_next = beta_two * square + (1.0 - beta_two) * gradient * gradient
    scaled_moment = moment_next / (1.0 - beta_one**bias_steps)
    scaled_square = square_next / (1.0 - beta_two**bias_steps)
    change = scaled_moment / (jnp.sqrt(scaled_square) + epsilon) + weight_decay * weight
    return (weight - learn_rate * change, moment_next, square_next)


def on_device(
    tokens,
    cotangent,
    inner_weight,
    inner_mean,
    inner_square,
    outer_weight,
    outer_mean,
    outer_square,
):
    token_gradient, inner_gradient, outer_gradient = exchange(
        tokens.T, cotangent.T, inner_weight, outer_weight.T
    )
    inner = adam_step(inner_weight, inner_mean, inner_square, inner_gradient)
    outer = adam_step(outer_weight.T, outer_mean.T, outer_square.T, outer_gradient)
    return (token_gradient.T, *inner, *(array.T for array in outer))


def solution(mesh):
    grid = Mesh(mesh.devices.reshape(2, 4, 4, 2, 4), AXES)
    activation, inner, outer = P(ROW, COL), P(None, ROW, COL), P(COL, ROW)
    return jax.shard_map(
        on_device,
        mesh=grid,
        in_specs=(activation, activation, inner, inner, inner, outer, outer, outer),
        out_specs=(activation, inner, inner, inner, outer, outer, outer),
        check_vma=False,
    )
```
